32 devices in a mesh: gx: 2 (over x), gy: 4 (over y, core), gz: 4 (over z).
Axes of the slice: x: 2, y: 2, z: 4, core: 2. Of those that a mesh axis runs over, the one named last changes fastest.
Arguments:
- field: bfloat16 [81, 16, 64, 1024], P(None, 'gx', 'gy', 'gz'), may hold values from -6 to 6
- samples: int32 [3, 8, 131072], P(None, None, ('gx', 'gy', 'gz')), may hold values from 0 to 1023, as said below
- weights: float32 [8, 131072], P(None, ('gx', 'gy', 'gz')), may hold values from 0.05 to 0.25
- destination: int32 [2, 131072], P(None, ('gx', 'gy', 'gz')), may hold values from 0 to 127, as said below
- transfer: bfloat16 [81, 131072], P(None, ('gx', 'gy', 'gz')), may hold values from -5 to 5
Outputs:
- shadowed: bfloat16 [81, 131072], P(None, ('gx', 'gy', 'gz'))
The draws below stay inside these ranges and needn't reach their ends.
Inputs may be any that keep to these rules, and one draw needn't show every extreme that they name: Number the devices with gz fastest and gx slowest; device b holds grid cells b_x * 8 to (b_x + 1) * 8 - 1 along the first dimension and likewise along the others. Every sample of a receiver in the b-th block of 4096 receivers lies at most 2 cells, periodically along each dimension, outside device b's cells; samples[0] is below 16, samples[1] below 64, samples[2] below 1024. destination[0] is below 32 and destination[1] below 128. Of the b-th block of 4096 receivers exactly 128 have each value of destination[0], and those take each value of destination[1] once, so the columns of the output are a permutation of the receivers.
All inputs are finite; a program needn't handle non-finite values.
Results may differ from the reference program's by a relative error of at most 0.011.
Values may be sent and summed in bfloat16 or wider, within the bound.
A program may use at most 128 MiB of HBM per device.

```python
import math
import jax
import jax.numpy as jnp
from jax import lax

CX = 8
CY = 16
CZ = 256
RECV_DEV = 4096
HALO = 2
SAMPLES = 8
DEGREES = 9
POLAR = 32
AZIMUTH = 32
COEFFS = 81
NX = 16
NY = 64
NZ = 1024
RECEIVERS = 131072
PER_PAIR = 128
N_GX = 2
N_GY = 4
N_GZ = 4


def draw_samples(key, part):
    receiver = jnp.arange(RECEIVERS, dtype=jnp.int32)
    block = receiver // RECV_DEV
    block_x = block // (N_GY * N_GZ)
    block_y = block // N_GZ % N_GY
    block_z = block % N_GZ
    subkeys = jax.random.split(key, 3)
    offset_x = jax.random.randint(subkeys[0], (SAMPLES, RECEIVERS), -HALO, CX + HALO, dtype=jnp.int32)
    offset_y = jax.random.randint(subkeys[1], (SAMPLES, RECEIVERS), -HALO, CY + HALO, dtype=jnp.int32)
    offset_z = jax.random.randint(subkeys[2], (SAMPLES, RECEIVERS), -HALO, CZ + HALO, dtype=jnp.int32)
    coord_x = (block_x[None, :] * CX + offset_x) % NX
    coord_y = (block_y[None, :] * CY + offset_y) % NY
    coord_z = (block_z[None, :] * CZ + offset_z) % NZ
    return jnp.stack([coord_x, coord_y, coord_z]).astype(jnp.int32)


def draw_destination(key, part):
    devices = N_GX * N_GY * N_GZ
    scores = jax.random.randint(key, (devices, RECV_DEV), 0, 4096, dtype=jnp.int32) * RECV_DEV + jnp.arange(RECV_DEV, dtype=jnp.int32)[None, :]
    ordering = jnp.argsort(scores, axis=1, stable=True).astype(jnp.int32)
    owners = ordering // PER_PAIR
    inside = ordering % PER_PAIR
    return jnp.stack([owners.reshape(RECEIVERS), inside.reshape(RECEIVERS)]).astype(jnp.int32)


def level_of(own_key, dims, shards, least, high):
    def one(position, blocks):
        draws = jax.random.uniform(jax.random.fold_in(jax.random.fold_in(own_key, 6), position), (blocks,), jnp.float32, least / len(shards), high / len(shards))
        return jnp.repeat(jnp.exp(draws), dims[position] // blocks).reshape((-1,) + (1,) * (len(dims) - position - 1))

    level = one(*shards[0])
    for cut in shards[1:]:
        level = level * one(*cut)
    return level


def normal_values(key, dims, deviation, most, cuts=(), kind=jnp.bfloat16):
    loudness = level_of(key, dims, cuts, -0.22, 0.18) if cuts else 1.0
    array = jax.random.normal(key, dims, jnp.float32) * deviation * loudness
    return jnp.minimum(jnp.maximum(array, -most), most).astype(kind)


def setup_inputs(seed: int = 0) -> dict:
    seeds = jax.random.split(jax.random.key(seed), 6)
    return {
        "field": normal_values(seeds[0], (COEFFS, NX, NY, NZ), 1.0, 6.0, ((1, 2), (2, 4), (3, 4))),
        "samples": draw_samples(jax.random.fold_in(seeds[5], 71), 0),
        "weights": jnp.clip(0.05 + 0.2 * jax.random.uniform(seeds[2], (SAMPLES, RECEIVERS), jnp.float32) ** level_of(seeds[2], (SAMPLES, RECEIVERS), ((1, 32),), -0.2, 0.2), 0.05, 0.25),
        "destination": draw_destination(jax.random.fold_in(seeds[5], 71), 0),
        "transfer": normal_values(seeds[4], (COEFFS, RECEIVERS), 0.8, 5.0, ((1, 32),)),
    }


def harmonic_values(cosines, angles):
    sines = jnp.sqrt(jnp.maximum(1.0 - cosines * cosines, 0.0))
    entries = {}
    for azimuthal in range(DEGREES):
        diagonal_term = (-1.0) ** azimuthal * float(math.prod(range(1, 2 * azimuthal, 2))) * sines ** azimuthal
        legendre = {azimuthal: diagonal_term}
        if azimuthal + 1 < DEGREES:
            legendre[azimuthal + 1] = cosines * (2 * azimuthal + 1) * diagonal_term
        for degree in range(azimuthal + 2, DEGREES):
            legendre[degree] = ((2 * degree - 1) * cosines * legendre[degree - 1] - (degree + azimuthal - 1) * legendre[degree - 2]) / (degree - azimuthal)
        for degree in range(azimuthal, DEGREES):
            factor = math.sqrt((2 * degree + 1) / (4.0 * math.pi) * math.factorial(degree - azimuthal) / math.factorial(degree + azimuthal))
            if azimuthal == 0:
                entries[degree, 0] = factor * legendre[degree]
            else:
                entries[degree, azimuthal] = math.sqrt(2.0) * factor * jnp.cos(azimuthal * angles) * legendre[degree]
                entries[degree, -azimuthal] = math.sqrt(2.0) * factor * jnp.sin(azimuthal * angles) * legendre[degree]
    return jnp.stack([entries[degree, signed] for degree in range(DEGREES) for signed in range(-degree, degree + 1)])

def direction_tables():
    polar_cos = (jnp.arange(POLAR, dtype=jnp.float32) + 0.5) * (2.0 / POLAR) - 1.0
    beside_all = (jnp.arange(AZIMUTH, dtype=jnp.float32) + 0.5) * (2.0 * math.pi / AZIMUTH)
    cosines = jnp.repeat(polar_cos, AZIMUTH)
    angles = jnp.tile(beside_all, POLAR)
    values = harmonic_values(cosines, angles)
    basis = values.T.astype(jnp.bfloat16)
    projector = (values * (4.0 * math.pi / (POLAR * AZIMUTH))).astype(jnp.bfloat16)
    return (basis, projector)

def triple_product(transfer_block, shadow_block, basis, projector):
    transfer_dirs = jnp.dot(basis, transfer_block, preferred_element_type=jnp.float32)
    shadow_dirs = jnp.dot(basis, shadow_block, preferred_element_type=jnp.float32)
    product = (transfer_dirs * shadow_dirs).astype(jnp.bfloat16)
    return jnp.dot(projector, product, preferred_element_type=jnp.float32).astype(jnp.bfloat16)

def reference(field, samples, weights, destination, transfer):
    basis, projector = direction_tables()
    flat_field = field.reshape(COEFFS, NX * NY * NZ)
    blocks = RECEIVERS // RECV_DEV
    flat_index = ((samples[0] * NY + samples[1]) * NZ + samples[2]).astype(jnp.int32)

    def interpolate(index):
        start = (index * RECV_DEV).astype(jnp.int32)
        columns = lax.dynamic_slice_in_dim(flat_index, start, RECV_DEV, 1)
        block_weights = lax.dynamic_slice_in_dim(weights, start, RECV_DEV, 1)
        gathered = jnp.take(flat_field, columns.reshape(-1), axis=1).reshape(COEFFS, SAMPLES, RECV_DEV)
        return lax.optimization_barrier(jnp.sum(gathered.astype(jnp.float32) * block_weights[None].astype(jnp.float32), axis=1)).astype(jnp.bfloat16)
    pieces = lax.map(interpolate, jnp.arange(blocks, dtype=jnp.int32))
    visibility = jnp.transpose(pieces, (1, 0, 2)).reshape(COEFFS, RECEIVERS)
    source_block = jnp.arange(RECEIVERS, dtype=jnp.int32) // RECV_DEV
    columns_out = (destination[0] * RECV_DEV + source_block * PER_PAIR + destination[1]).astype(jnp.int32)
    routed = jnp.zeros((COEFFS, RECEIVERS), jnp.bfloat16).at[:, columns_out].set(visibility)

    def relight(index):
        start = (index * RECV_DEV).astype(jnp.int32)
        transfer_block = lax.dynamic_slice_in_dim(transfer, start, RECV_DEV, 1)
        shadow_block = lax.dynamic_slice_in_dim(routed, start, RECV_DEV, 1)
        return triple_product(transfer_block, shadow_block, basis, projector)
    results = lax.map(relight, jnp.arange(blocks, dtype=jnp.int32))
    return jnp.transpose(results, (1, 0, 2)).reshape(COEFFS, RECEIVERS)
```

```python
import functools
import math

import jax
import jax.numpy as jnp
import numpy as np
from jax import lax
from jax.experimental import pallas as pl
from jax.experimental.pallas import tpu as pltpu
from jax.sharding import PartitionSpec as P

HALO = 2
DEGREES = 9
POLAR = 32
AZIMUTH = 32
GROUP = 8
LANES = 128


def harmonic_values(cosines, angles):
    f32 = np.float32
    sines = np.sqrt(np.maximum(f32(1.0) - cosines * cosines, f32(0.0)))
    entries = {}
    for azimuthal in range(DEGREES):
        diagonal_term = (
            f32((-1.0) ** azimuthal * float(math.prod(range(1, 2 * azimuthal, 2))))
            * sines**azimuthal
        ).astype(f32)
        legendre = {azimuthal: diagonal_term}
        if azimuthal + 1 < DEGREES:
            legendre[azimuthal + 1] = cosines * f32(2 * azimuthal + 1) * diagonal_term
        for degree in range(azimuthal + 2, DEGREES):
            legendre[degree] = (
                f32(2 * degree - 1) * cosines * legendre[degree - 1]
                - f32(degree + azimuthal - 1) * legendre[degree - 2]
            ) / f32(degree - azimuthal)
        for degree in range(azimuthal, DEGREES):
            factor = math.sqrt(
                (2 * degree + 1)
                / (4.0 * math.pi)
                * math.factorial(degree - azimuthal)
                / math.factorial(degree + azimuthal)
            )
            if azimuthal == 0:
                entries[degree, 0] = f32(factor) * legendre[degree]
            else:
                scale = f32(math.sqrt(2.0) * factor)
                turned = f32(azimuthal) * angles
                entries[degree, azimuthal] = scale * np.cos(turned) * legendre[degree]
                entries[degree, -azimuthal] = scale * np.sin(turned) * legendre[degree]
    return np.stack(
        [
            entries[degree, signed]
            for degree in range(DEGREES)
            for signed in range(-degree, degree + 1)
        ]
    ).astype(f32)


def direction_tables():
    f32 = np.float32
    polar_cos = (np.arange(POLAR, dtype=f32) + f32(0.5)) * f32(2.0 / POLAR) - f32(1.0)
    beside_all = (np.arange(AZIMUTH, dtype=f32) + f32(0.5)) * f32(2.0 * math.pi / AZIMUTH)
    values = harmonic_values(np.repeat(polar_cos, AZIMUTH), np.tile(beside_all, POLAR))
    basis = values.T.astype(jnp.bfloat16)
    projector = (values * f32(4.0 * math.pi / (POLAR * AZIMUTH))).astype(jnp.bfloat16)
    return jnp.asarray(basis), jnp.asarray(projector)


def round_up(n, m):
    return -(-n // m) * m


def gather_kernel(dims, cells_ref, slots_ref, weights_ref, field_ref, beside_ref, edge_ref,
                  own_ref, other_ref, table, plane, beside, rows):
    coeffs, cells_x, cells_y, cells_z, beside_y, pitch_y, pitch_z, count, passes, samples = dims
    step = pl.program_id(0)
    padded = round_up(coeffs, 8)

    @pl.when(step == 0)
    def _():
        if padded > coeffs:
            plane[:, coeffs * cells_y :, :] = jnp.zeros_like(plane[:, coeffs * cells_y :, :])
            beside[:, coeffs * beside_y :, :] = jnp.zeros_like(beside[:, coeffs * beside_y :, :])

    @pl.when(step < cells_x)
    def _():
        start = step * (pitch_y * pitch_z)
        for part in range(cells_z // LANES):
            lanes = pl.ds(part * LANES, LANES)
            block = field_ref[:, 0, :, lanes].astype(jnp.float32)
            plane[part, : coeffs * cells_y, :] = block.reshape(coeffs * cells_y, LANES)
            block = beside_ref[:, 0, :, lanes].astype(jnp.float32)
            beside[part, : coeffs * beside_y, :] = block.reshape(coeffs * beside_y, LANES)
        for part in range(cells_z // LANES):
            for y in range(cells_y + 2 * HALO):
                if y < cells_y:
                    line = plane[part, pl.ds(y, padded, stride=cells_y), :]
                else:
                    line = beside[part, pl.ds(y - cells_y, padded, stride=beside_y), :]
                at = pl.multiple_of(start + y * pitch_z + part * LANES, 8)
                table[pl.ds(at, LANES), :padded] = line.T
        for y in range(cells_y + 2 * HALO):
            at = pl.multiple_of(start + y * pitch_z + cells_z, 8)
            table[pl.ds(at, 8), :coeffs] = edge_ref[0, 8 * y : 8 * y + 8, :]

    @pl.when(step == cells_x)
    def _():
        sublane = lax.broadcasted_iota(jnp.int32, (GROUP, LANES), 0)
        masks = [sublane == k for k in range(GROUP)]
        for which in range(passes):

            def group(g, carry):
                first = pl.multiple_of(g * GROUP, GROUP)
                scale = weights_ref[which, pl.ds(first, GROUP), :]
                total = jnp.zeros((GROUP, LANES), jnp.float32)
                for s in range(samples):
                    base = (which * samples + s) * count + first
                    merged = table[pl.ds(cells_ref[base], GROUP, stride=0), :]
                    for k in range(1, GROUP):
                        row = table[pl.ds(cells_ref[base + k], GROUP, stride=0), :]
                        merged = jnp.where(masks[k], row, merged)
                    total = total + merged * scale[:, s : s + 1]
                for k in range(GROUP):
                    slot = slots_ref[which * count + first + k]
                    rows[pl.ds(slot, 1), :] = total[k : k + 1, :]
                return carry

            lax.fori_loop(0, count // GROUP, group, 0)

            def turn(b, carry):
                at = pl.multiple_of(b * LANES, LANES)
                turned = rows[pl.ds(at, LANES), :].T[:coeffs, :]
                if which == 0:
                    own_ref[:, pl.ds(at, LANES)] = turned
                else:
                    other_ref[which - 1, :, pl.ds(at, LANES)] = turned.astype(jnp.bfloat16)
                return carry

            lax.fori_loop(0, count // LANES, turn, 0)


def shifted(value, axis, by):
    count = lax.axis_size(axis)
    return lax.ppermute(value, axis, [((i + by) % count, i) for i in range(count)])


def per_device(field, samples, weights, destination, transfer):
    basis, projector = direction_tables()
    coeffs, cells_x, cells_y, cells_z = field.shape
    count = transfer.shape[1]
    reach = samples.shape[1]
    along = [lax.axis_size(a) for a in ("gx", "gy", "gz")]
    devices = math.prod(along)
    per_pair = count // devices
    pitch_y = cells_y + 2 * HALO
    pitch_z = round_up(cells_z + 2 * HALO, 8)
    beside_y = 8
    plane_cells = pitch_y * pitch_z

    def local(coord, axis, cells):
        whole = cells * lax.axis_size(axis)
        at = (coord - lax.axis_index(axis) * cells) % whole
        return jnp.where(at >= cells + HALO, at - whole + cells + 2 * HALO, at)

    local_y = local(samples[1], "gy", cells_y)
    local_z = local(samples[2], "gz", cells_z)
    packed = samples[0] * plane_cells + local_y * pitch_z + local_z
    slot = destination[0] * per_pair + destination[1]
    offsets = sorted({0, 1 % along[0], (along[0] - 1) % along[0]})
    listed = jnp.concatenate([packed, slot[None]], axis=0)
    lists, scales = [listed], [weights]
    for by in offsets[1:]:
        lists.append(shifted(listed, "gx", by))
        scales.append(shifted(weights, "gx", by))

    beside = jnp.concatenate(
        [
            shifted(field[:, :, :HALO, :], "gy", 1),
            shifted(field[:, :, cells_y - HALO :, :], "gy", -1),
            jnp.zeros((coeffs, cells_x, beside_y - 2 * HALO, cells_z), field.dtype),
        ],
        axis=2,
    )
    low_z = field[:, :, :, :HALO].transpose(1, 2, 3, 0)
    high_z = field[:, :, :, cells_z - HALO :].transpose(1, 2, 3, 0)
    edge = jnp.concatenate([shifted(low_z, "gz", 1), shifted(high_z, "gz", -1)], axis=2)
    edge = jnp.concatenate(
        [edge, shifted(edge[:, :HALO], "gy", 1), shifted(edge[:, cells_y - HALO :], "gy", -1)],
        axis=1,
    )
    edge = jnp.pad(edge.astype(jnp.float32), ((0, 0), (0, 0), (0, 8 - 2 * HALO), (0, 0)))
    edge = edge.reshape(cells_x, pitch_y * 8, coeffs)

    first = lax.axis_index("gx") * cells_x
    cells, slots, factors = [], [], []
    for part, scale in zip(lists, scales):
        at = part[:reach] - first * plane_cells
        mine = (at >= 0) & (at < cells_x * plane_cells)
        cells.append(jnp.where(mine, at, 0).reshape(-1))
        slots.append(part[reach])
        factors.append(jnp.where(mine, scale, 0.0).T)
    passes = len(offsets)
    dims = (coeffs, cells_x, cells_y, cells_z, beside_y, pitch_y, pitch_z, count, passes, reach)
    last = cells_x - 1
    others = max(passes - 1, 1)
    own, other = pl.pallas_call(
        functools.partial(gather_kernel, dims),
        grid=(cells_x + 1,),
        in_specs=[
            pl.BlockSpec(memory_space=pltpu.SMEM),
            pl.BlockSpec(memory_space=pltpu.SMEM),
            pl.BlockSpec((passes, count, reach), lambda i: (0, 0, 0)),
            pl.BlockSpec((coeffs, 1, cells_y, cells_z), lambda i: (0, jnp.minimum(i, last), 0, 0)),
            pl.BlockSpec((coeffs, 1, beside_y, cells_z), lambda i: (0, jnp.minimum(i, last), 0, 0)),
            pl.BlockSpec((1, pitch_y * 8, coeffs), lambda i: (jnp.minimum(i, last), 0, 0)),
        ],
        out_specs=[
            pl.BlockSpec((coeffs, count), lambda i: (0, 0)),
            pl.BlockSpec((others, coeffs, count), lambda i: (0, 0, 0)),
        ],
        out_shape=[
            jax.ShapeDtypeStruct((coeffs, count), jnp.float32),
            jax.ShapeDtypeStruct((others, coeffs, count), jnp.bfloat16),
        ],
        scratch_shapes=[
            pltpu.VMEM((cells_x * plane_cells + 8, LANES), jnp.float32),
            pltpu.VMEM((cells_z // LANES, round_up(coeffs, 8) * cells_y, LANES), jnp.float32),
            pltpu.VMEM((cells_z // LANES, round_up(coeffs, 8) * beside_y, LANES), jnp.float32),
            pltpu.VMEM((count, LANES), jnp.float32),
        ],
        compiler_params=pltpu.CompilerParams(vmem_limit_bytes=60 * 1024 * 1024),
    )(
        jnp.concatenate(cells),
        jnp.concatenate(slots),
        jnp.stack(factors),
        field,
        beside,
        edge,
    )
    total = own
    for i, by in enumerate(offsets[1:]):
        total = total + shifted(other[i], "gx", -by).astype(jnp.float32)
    outgoing = total.astype(jnp.bfloat16)
    routed = lax.all_to_all(outgoing, ("gx", "gy", "gz"), split_axis=1, concat_axis=1, tiled=True)

    block = min(2048, count)
    results = []
    for start in range(0, count, block):
        columns = slice(start, start + block)
        transfer_dirs = jnp.dot(basis, transfer[:, columns], preferred_element_type=jnp.float32)
        shadow_dirs = jnp.dot(basis, routed[:, columns], preferred_element_type=jnp.float32)
        product = (transfer_dirs * shadow_dirs).astype(jnp.bfloat16)
        results.append(
            jnp.dot(projector, product, preferred_element_type=jnp.float32).astype(jnp.bfloat16)
        )
    return jnp.concatenate(results, axis=1)


def solution(mesh):
    placed = (
        P(None, "gx", "gy", "gz"),
        P(None, None, ("gx", "gy", "gz")),
        P(None, ("gx", "gy", "gz")),
        P(None, ("gx", "gy", "gz")),
        P(None, ("gx", "gy", "gz")),
    )
    return jax.shard_map(
        per_device,
        mesh=mesh,
        in_specs=placed,
        out_specs=P(None, ("gx", "gy", "gz")),
        check_vma=False,
    )
```

```python
import functools
import math

import jax
import jax.numpy as jnp
import numpy as np
from jax import lax
from jax.experimental import pallas as pl
from jax.experimental.pallas import tpu as pltpu
from jax.sharding import PartitionSpec as P

HALO = 2
DEGREES = 9
POLAR = 32
AZIMUTH = 32
GROUP = 8
LANES = 128


def harmonic_values(cosines, angles):
    f32 = np.float32
    sines = np.sqrt(np.maximum(f32(1.0) - cosines * cosines, f32(0.0)))
    entries = {}
    for azimuthal in range(DEGREES):
        diagonal_term = (
            f32((-1.0) ** azimuthal * float(math.prod(range(1, 2 * azimuthal, 2))))
            * sines**azimuthal
        ).astype(f32)
        legendre = {azimuthal: diagonal_term}
        if azimuthal + 1 < DEGREES:
            legendre[azimuthal + 1] = cosines * f32(2 * azimuthal + 1) * diagonal_term
        for degree in range(azimuthal + 2, DEGREES):
            legendre[degree] = (
                f32(2 * degree - 1) * cosines * legendre[degree - 1]
                - f32(degree + azimuthal - 1) * legendre[degree - 2]
            ) / f32(degree - azimuthal)
        for degree in range(azimuthal, DEGREES):
            factor = math.sqrt(
                (2 * degree + 1)
                / (4.0 * math.pi)
                * math.factorial(degree - azimuthal)
                / math.factorial(degree + azimuthal)
            )
            if azimuthal == 0:
                entries[degree, 0] = f32(factor) * legendre[degree]
            else:
                scale = f32(math.sqrt(2.0) * factor)
                turned = f32(azimuthal) * angles
                entries[degree, azimuthal] = scale * np.cos(turned) * legendre[degree]
                entries[degree, -azimuthal] = scale * np.sin(turned) * legendre[degree]
    return np.stack(
        [
            entries[degree, signed]
            for degree in range(DEGREES)
            for signed in range(-degree, degree + 1)
        ]
    ).astype(f32)


def direction_tables():
    f32 = np.float32
    polar_cos = (np.arange(POLAR, dtype=f32) + f32(0.5)) * f32(2.0 / POLAR) - f32(1.0)
    beside_all = (np.arange(AZIMUTH, dtype=f32) + f32(0.5)) * f32(2.0 * math.pi / AZIMUTH)
    values = harmonic_values(np.repeat(polar_cos, AZIMUTH), np.tile(beside_all, POLAR))
    basis = values.T.astype(jnp.bfloat16)
    projector = (values * f32(4.0 * math.pi / (POLAR * AZIMUTH))).astype(jnp.bfloat16)
    return jnp.asarray(basis), jnp.asarray(projector)


def round_up(n, m):
    return -(-n // m) * m


def gather_kernel(dims, cells_ref, slots_ref, weights_ref, field_ref, beside_ref, edge_ref,
                  own_ref, other_ref, table, plane, beside, rows, partial):
    coeffs, cells_x, cells_y, cells_z, beside_y, pitch_y, pitch_z, count, passes, samples = dims
    step = pl.program_id(0)
    padded = round_up(coeffs, 8)

    @pl.when(step == 0)
    def _():
        if padded > coeffs:
            plane[:, coeffs * cells_y :, :] = jnp.zeros_like(plane[:, coeffs * cells_y :, :])
            beside[:, coeffs * beside_y :, :] = jnp.zeros_like(beside[:, coeffs * beside_y :, :])

    @pl.when(step < cells_x)
    def _():
        start = step * (pitch_y * pitch_z)
        for part in range(cells_z // LANES):
            lanes = pl.ds(part * LANES, LANES)
            block = field_ref[:, 0, :, lanes].astype(jnp.float32)
            plane[part, : coeffs * cells_y, :] = block.reshape(coeffs * cells_y, LANES)
            block = beside_ref[:, 0, :, lanes].astype(jnp.float32)
            beside[part, : coeffs * beside_y, :] = block.reshape(coeffs * beside_y, LANES)
        for part in range(cells_z // LANES):
            for y in range(cells_y + 2 * HALO):
                if y < cells_y:
                    line = plane[part, pl.ds(y, padded, stride=cells_y), :]
                else:
                    line = beside[part, pl.ds(y - cells_y, padded, stride=beside_y), :]
                at = pl.multiple_of(start + y * pitch_z + part * LANES, 8)
                table[pl.ds(at, LANES), :padded] = line.T
        for y in range(cells_y + 2 * HALO):
            at = pl.multiple_of(start + y * pitch_z + cells_z, 8)
            table[pl.ds(at, 8), :coeffs] = edge_ref[0, 8 * y : 8 * y + 8, :]

    @pl.when(step == cells_x)
    def _():
        sublane = lax.broadcasted_iota(jnp.int32, (GROUP, LANES), 0)
        masks = [sublane == k for k in range(GROUP)]
        for which in range(passes):

            split = 1
            share = samples // split
            for piece in range(split):
                final = piece == split - 1

                def load(g):
                    merged = []
                    for s in range(piece * share, (piece + 1) * share):
                        base = (which * samples + s) * count + g * GROUP
                        near = cells_ref.at[pl.ds(pl.multiple_of(base, GROUP), GROUP)]
                        value = table[pl.ds(near[0], GROUP, stride=0), :]
                        for k in range(1, GROUP):
                            row = table[pl.ds(near[k], GROUP, stride=0), :]
                            value = jnp.where(masks[k], row, value)
                        merged.append(value)
                    return tuple(merged)

                def finish(g, merged):
                    first = pl.multiple_of(g * GROUP, GROUP)
                    scale = weights_ref[which, pl.ds(first, GROUP), :]
                    total = merged[0] * scale[:, piece * share : piece * share + 1]
                    for s in range(1, share):
                        at = piece * share + s
                        total = total + merged[s] * scale[:, at : at + 1]
                    if piece > 0:
                        total = total + partial[pl.ds(first, GROUP), :]
                    if not final:
                        partial[pl.ds(first, GROUP), :] = total
                        return
                    ahead = slots_ref.at[pl.ds(pl.multiple_of(which * count + first, GROUP), GROUP)]
                    for k in range(GROUP):
                        rows[pl.ds(ahead[k], 1), :] = total[k : k + 1, :]

                def advance(g, merged):
                    finish(g - 1, merged)
                    return load(g)

                finish(count // GROUP - 1, lax.fori_loop(1, count // GROUP, advance, load(0)))

            def turn(b, carry):
                at = pl.multiple_of(b * LANES, LANES)
                turned = rows[pl.ds(at, LANES), :].T[:coeffs, :]
                if which == 0:
                    own_ref[:, pl.ds(at, LANES)] = turned
                else:
                    other_ref[which - 1, :, pl.ds(at, LANES)] = turned.astype(jnp.bfloat16)
                return carry

            lax.fori_loop(0, count // LANES, turn, 0)


def shifted(value, axis, by):
    count = lax.axis_size(axis)
    return lax.ppermute(value, axis, [((i + by) % count, i) for i in range(count)])


def per_device(field, samples, weights, destination, transfer):
    basis, projector = direction_tables()
    coeffs, cells_x, cells_y, cells_z = field.shape
    count = transfer.shape[1]
    reach = samples.shape[1]
    along = [lax.axis_size(a) for a in ("gx", "gy", "gz")]
    devices = math.prod(along)
    per_pair = count // devices
    pitch_y = cells_y + 2 * HALO
    pitch_z = round_up(cells_z + 2 * HALO, 8)
    beside_y = 8
    plane_cells = pitch_y * pitch_z

    def local(coord, axis, cells):
        whole = cells * lax.axis_size(axis)
        at = (coord - lax.axis_index(axis) * cells) % whole
        return jnp.where(at >= cells + HALO, at - whole + cells + 2 * HALO, at)

    local_y = local(samples[1], "gy", cells_y)
    local_z = local(samples[2], "gz", cells_z)
    packed = samples[0] * plane_cells + local_y * pitch_z + local_z
    slot = destination[0] * per_pair + destination[1]
    offsets = sorted({0, 1 % along[0], (along[0] - 1) % along[0]})
    listed = jnp.concatenate([packed, slot[None]], axis=0)
    lists, scales = [listed], [weights]
    for by in offsets[1:]:
        lists.append(shifted(listed, "gx", by))
        scales.append(shifted(weights, "gx", by))

    beside = jnp.concatenate(
        [
            shifted(field[:, :, :HALO, :], "gy", 1),
            shifted(field[:, :, cells_y - HALO :, :], "gy", -1),
            jnp.zeros((coeffs, cells_x, beside_y - 2 * HALO, cells_z), field.dtype),
        ],
        axis=2,
    )
    low_z = field[:, :, :, :HALO].transpose(1, 2, 3, 0)
    high_z = field[:, :, :, cells_z - HALO :].transpose(1, 2, 3, 0)
    edge = jnp.concatenate([shifted(low_z, "gz", 1), shifted(high_z, "gz", -1)], axis=2)
    edge = jnp.concatenate(
        [edge, shifted(edge[:, :HALO], "gy", 1), shifted(edge[:, cells_y - HALO :], "gy", -1)],
        axis=1,
    )
    edge = jnp.pad(edge.astype(jnp.float32), ((0, 0), (0, 0), (0, 8 - 2 * HALO), (0, 0)))
    edge = edge.reshape(cells_x, pitch_y * 8, coeffs)

    first = lax.axis_index("gx") * cells_x
    cells, slots, factors = [], [], []
    for part, scale in zip(lists, scales):
        at = part[:reach] - first * plane_cells
        mine = (at >= 0) & (at < cells_x * plane_cells)
        cells.append(jnp.where(mine, at, 0).reshape(-1))
        slots.append(part[reach])
        factors.append(jnp.where(mine, scale, 0.0).T)
    passes = len(offsets)
    dims = (coeffs, cells_x, cells_y, cells_z, beside_y, pitch_y, pitch_z, count, passes, reach)
    last = cells_x - 1
    others = max(passes - 1, 1)
    own, other = pl.pallas_call(
        functools.partial(gather_kernel, dims),
        grid=(cells_x + 1,),
        in_specs=[
            pl.BlockSpec(memory_space=pltpu.SMEM),
            pl.BlockSpec(memory_space=pltpu.SMEM),
            pl.BlockSpec((passes, count, reach), lambda i: (0, 0, 0)),
            pl.BlockSpec((coeffs, 1, cells_y, cells_z), lambda i: (0, jnp.minimum(i, last), 0, 0)),
            pl.BlockSpec((coeffs, 1, beside_y, cells_z), lambda i: (0, jnp.minimum(i, last), 0, 0)),
            pl.BlockSpec((1, pitch_y * 8, coeffs), lambda i: (jnp.minimum(i, last), 0, 0)),
        ],
        out_specs=[
            pl.BlockSpec((coeffs, count), lambda i: (0, 0)),
            pl.BlockSpec((others, coeffs, count), lambda i: (0, 0, 0)),
        ],
        out_shape=[
            jax.ShapeDtypeStruct((coeffs, count), jnp.float32),
            jax.ShapeDtypeStruct((others, coeffs, count), jnp.bfloat16),
        ],
        scratch_shapes=[
            pltpu.VMEM((cells_x * plane_cells + 8, LANES), jnp.float32),
            pltpu.VMEM((cells_z // LANES, round_up(coeffs, 8) * cells_y, LANES), jnp.float32),
            pltpu.VMEM((cells_z // LANES, round_up(coeffs, 8) * beside_y, LANES), jnp.float32),
            pltpu.VMEM((count, LANES), jnp.float32),
            pltpu.VMEM((count, LANES), jnp.float32),
        ],
        compiler_params=pltpu.CompilerParams(vmem_limit_bytes=60 * 1024 * 1024),
    )(
        jnp.concatenate(cells),
        jnp.concatenate(slots),
        jnp.stack(factors),
        field,
        beside,
        edge,
    )
    total = own
    for i, by in enumerate(offsets[1:]):
        total = total + shifted(other[i], "gx", -by).astype(jnp.float32)
    outgoing = total.astype(jnp.bfloat16)
    routed = lax.all_to_all(outgoing, ("gx", "gy", "gz"), split_axis=1, concat_axis=1, tiled=True)

    block = min(2048, count)
    results = []
    for start in range(0, count, block):
        columns = slice(start, start + block)
        transfer_dirs = jnp.dot(basis, transfer[:, columns], preferred_element_type=jnp.float32)
        shadow_dirs = jnp.dot(basis, routed[:, columns], preferred_element_type=jnp.float32)
        product = (transfer_dirs * shadow_dirs).astype(jnp.bfloat16)
        results.append(
            jnp.dot(projector, product, preferred_element_type=jnp.float32).astype(jnp.bfloat16)
        )
    return jnp.concatenate(results, axis=1)


def solution(mesh):
    placed = (
        P(None, "gx", "gy", "gz"),
        P(None, None, ("gx", "gy", "gz")),
        P(None, ("gx", "gy", "gz")),
        P(None, ("gx", "gy", "gz")),
        P(None, ("gx", "gy", "gz")),
    )
    return jax.shard_map(
        per_device,
        mesh=mesh,
        in_specs=placed,
        out_specs=P(None, ("gx", "gy", "gz")),
        check_vma=False,
    )
```

```python
import functools
import math

import jax
import jax.numpy as jnp
import numpy as np
from jax import lax
from jax.experimental import pallas as pl
from jax.experimental.pallas import tpu as pltpu
from jax.sharding import PartitionSpec as P

HALO = 2
DEGREES = 9
POLAR = 32
AZIMUTH = 32
GROUP = 8
LANES = 128


def harmonic_values(cosines, angles):
    f32 = np.float32
    sines = np.sqrt(np.maximum(f32(1.0) - cosines * cosines, f32(0.0)))
    entries = {}
    for azimuthal in range(DEGREES):
        diagonal_term = (
            f32((-1.0) ** azimuthal * float(math.prod(range(1, 2 * azimuthal, 2))))
            * sines**azimuthal
        ).astype(f32)
        legendre = {azimuthal: diagonal_term}
        if azimuthal + 1 < DEGREES:
            legendre[azimuthal + 1] = cosines * f32(2 * azimuthal + 1) * diagonal_term
        for degree in range(azimuthal + 2, DEGREES):
            legendre[degree] = (
                f32(2 * degree - 1) * cosines * legendre[degree - 1]
                - f32(degree + azimuthal - 1) * legendre[degree - 2]
            ) / f32(degree - azimuthal)
        for degree in range(azimuthal, DEGREES):
            factor = math.sqrt(
                (2 * degree + 1)
                / (4.0 * math.pi)
                * math.factorial(degree - azimuthal)
                / math.factorial(degree + azimuthal)
            )
            if azimuthal == 0:
                entries[degree, 0] = f32(factor) * legendre[degree]
            else:
                scale = f32(math.sqrt(2.0) * factor)
                turned = f32(azimuthal) * angles
                entries[degree, azimuthal] = scale * np.cos(turned) * legendre[degree]
                entries[degree, -azimuthal] = scale * np.sin(turned) * legendre[degree]
    return np.stack(
        [
            entries[degree, signed]
            for degree in range(DEGREES)
            for signed in range(-degree, degree + 1)
        ]
    ).astype(f32)


def direction_tables():
    f32 = np.float32
    polar_cos = (np.arange(POLAR, dtype=f32) + f32(0.5)) * f32(2.0 / POLAR) - f32(1.0)
    beside_all = (np.arange(AZIMUTH, dtype=f32) + f32(0.5)) * f32(2.0 * math.pi / AZIMUTH)
    values = harmonic_values(np.repeat(polar_cos, AZIMUTH), np.tile(beside_all, POLAR))
    basis = values.T.astype(jnp.bfloat16)
    projector = (values * f32(4.0 * math.pi / (POLAR * AZIMUTH))).astype(jnp.bfloat16)
    return jnp.asarray(basis), jnp.asarray(projector)


def round_up(n, m):
    return -(-n // m) * m


def gather_kernel(dims, cells_ref, slots_ref, weights_ref, field_ref, beside_ref, edge_ref,
                  own_ref, other_ref, table, plane, beside, rows, staged, summed):
    coeffs, cells_x, cells_y, cells_z, beside_y, pitch_y, pitch_z, count, passes, samples = dims
    step = pl.program_id(0)
    padded = round_up(coeffs, 8)

    @pl.when(step == 0)
    def _():
        if padded > coeffs:
            plane[:, coeffs * cells_y :, :] = jnp.zeros_like(plane[:, coeffs * cells_y :, :])
            beside[:, coeffs * beside_y :, :] = jnp.zeros_like(beside[:, coeffs * beside_y :, :])

    @pl.when(step < cells_x)
    def _():
        start = step * (pitch_y * pitch_z)
        for part in range(cells_z // LANES):
            lanes = pl.ds(part * LANES, LANES)
            block = field_ref[:, 0, :, lanes].astype(jnp.float32)
            plane[part, : coeffs * cells_y, :] = block.reshape(coeffs * cells_y, LANES)
            block = beside_ref[:, 0, :, lanes].astype(jnp.float32)
            beside[part, : coeffs * beside_y, :] = block.reshape(coeffs * beside_y, LANES)
        for part in range(cells_z // LANES):
            for y in range(cells_y + 2 * HALO):
                if y < cells_y:
                    line = plane[part, pl.ds(y, padded, stride=cells_y), :]
                else:
                    line = beside[part, pl.ds(y - cells_y, padded, stride=beside_y), :]
                at = pl.multiple_of(start + y * pitch_z + part * LANES, 8)
                table[pl.ds(at, LANES), :padded] = line.T
        for y in range(cells_y + 2 * HALO):
            at = pl.multiple_of(start + y * pitch_z + cells_z, 8)
            table[pl.ds(at, 8), :coeffs] = edge_ref[0, 8 * y : 8 * y + 8, :]

    @pl.when(step == cells_x)
    def _():
        sublane = lax.broadcasted_iota(jnp.int32, (GROUP, LANES), 0)
        masks = [sublane == k for k in range(GROUP)]
        square = (LANES, LANES)
        diagonal = lax.broadcasted_iota(jnp.int32, square, 0) == lax.broadcasted_iota(
            jnp.int32, square, 1
        )
        for which in range(passes):

            groups = LANES // GROUP

            def scatter(block, g):
                base = pl.multiple_of(which * count + block * LANES + g * GROUP, GROUP)
                ahead = slots_ref.at[pl.ds(base, GROUP)]
                done = summed[pl.ds(pl.multiple_of(g * GROUP, GROUP), GROUP), :]
                for k in range(GROUP):
                    rows[pl.ds(ahead[k], 1), :] = done[k : k + 1, :]

            def receivers(block, carry):
                before = jnp.maximum(block - 1, 0)

                def group(g, inner):
                    scatter(before, g)
                    for s in range(samples):
                        base = (which * samples + s) * count + block * LANES + g * GROUP
                        near = cells_ref.at[pl.ds(pl.multiple_of(base, GROUP), GROUP)]
                        value = table[pl.ds(near[0], GROUP, stride=0), :]
                        for k in range(1, GROUP):
                            row = table[pl.ds(near[k], GROUP, stride=0), :]
                            value = jnp.where(masks[k], row, value)
                        staged[s, pl.ds(pl.multiple_of(g * GROUP, GROUP), GROUP), :] = value
                    return inner

                lax.fori_loop(0, groups, group, 0)
                total = jnp.zeros((LANES, LANES), jnp.float32)
                lanes = pl.ds(pl.multiple_of(block * LANES, LANES), LANES)
                for s in range(samples):
                    scale = jnp.where(diagonal, weights_ref[which, s : s + 1, lanes], 0.0)
                    high = scale.astype(jnp.bfloat16)
                    low = (scale - high.astype(jnp.float32)).astype(jnp.bfloat16)
                    value = staged[s].astype(jnp.bfloat16)
                    total = total + jnp.dot(high, value, preferred_element_type=jnp.float32)
                    total = total + jnp.dot(low, value, preferred_element_type=jnp.float32)
                summed[...] = total
                return carry

            lax.fori_loop(0, count // LANES, receivers, 0)

            def remain(g, carry):
                scatter(count // LANES - 1, g)
                return carry

            lax.fori_loop(0, groups, remain, 0)

            def turn(b, carry):
                at = pl.multiple_of(b * LANES, LANES)
                turned = rows[pl.ds(at, LANES), :].T[:coeffs, :]
                if which == 0:
                    own_ref[:, pl.ds(at, LANES)] = turned
                else:
                    other_ref[which - 1, :, pl.ds(at, LANES)] = turned.astype(jnp.bfloat16)
                return carry

            lax.fori_loop(0, count // LANES, turn, 0)


def shifted(value, axis, by):
    count = lax.axis_size(axis)
    return lax.ppermute(value, axis, [((i + by) % count, i) for i in range(count)])


def per_device(field, samples, weights, destination, transfer):
    basis, projector = direction_tables()
    coeffs, cells_x, cells_y, cells_z = field.shape
    count = transfer.shape[1]
    reach = samples.shape[1]
    along = [lax.axis_size(a) for a in ("gx", "gy", "gz")]
    devices = math.prod(along)
    per_pair = count // devices
    pitch_y = cells_y + 2 * HALO
    pitch_z = round_up(cells_z + 2 * HALO, 8)
    beside_y = 8
    plane_cells = pitch_y * pitch_z

    def local(coord, axis, cells):
        whole = cells * lax.axis_size(axis)
        at = (coord - lax.axis_index(axis) * cells) % whole
        return jnp.where(at >= cells + HALO, at - whole + cells + 2 * HALO, at)

    local_y = local(samples[1], "gy", cells_y)
    local_z = local(samples[2], "gz", cells_z)
    packed = samples[0] * plane_cells + local_y * pitch_z + local_z
    slot = destination[0] * per_pair + destination[1]
    offsets = sorted({0, 1 % along[0], (along[0] - 1) % along[0]})
    listed = jnp.concatenate([packed, slot[None]], axis=0)
    lists, scales = [listed], [weights]
    for by in offsets[1:]:
        lists.append(shifted(listed, "gx", by))
        scales.append(shifted(weights, "gx", by))

    beside = jnp.concatenate(
        [
            shifted(field[:, :, :HALO, :], "gy", 1),
            shifted(field[:, :, cells_y - HALO :, :], "gy", -1),
            jnp.zeros((coeffs, cells_x, beside_y - 2 * HALO, cells_z), field.dtype),
        ],
        axis=2,
    )
    low_z = field[:, :, :, :HALO].transpose(1, 2, 3, 0)
    high_z = field[:, :, :, cells_z - HALO :].transpose(1, 2, 3, 0)
    edge = jnp.concatenate([shifted(low_z, "gz", 1), shifted(high_z, "gz", -1)], axis=2)
    edge = jnp.concatenate(
        [edge, shifted(edge[:, :HALO], "gy", 1), shifted(edge[:, cells_y - HALO :], "gy", -1)],
        axis=1,
    )
    edge = jnp.pad(edge.astype(jnp.float32), ((0, 0), (0, 0), (0, 8 - 2 * HALO), (0, 0)))
    edge = edge.reshape(cells_x, pitch_y * 8, coeffs)

    first = lax.axis_index("gx") * cells_x
    cells, slots, factors = [], [], []
    for part, scale in zip(lists, scales):
        at = part[:reach] - first * plane_cells
        mine = (at >= 0) & (at < cells_x * plane_cells)
        cells.append(jnp.where(mine, at, 0).reshape(-1))
        slots.append(part[reach])
        factors.append(jnp.where(mine, scale, 0.0))
    passes = len(offsets)
    dims = (coeffs, cells_x, cells_y, cells_z, beside_y, pitch_y, pitch_z, count, passes, reach)
    last = cells_x - 1
    others = max(passes - 1, 1)
    own, other = pl.pallas_call(
        functools.partial(gather_kernel, dims),
        grid=(cells_x + 1,),
        in_specs=[
            pl.BlockSpec(memory_space=pltpu.SMEM),
            pl.BlockSpec(memory_space=pltpu.SMEM),
            pl.BlockSpec((passes, reach, count), lambda i: (0, 0, 0)),
            pl.BlockSpec((coeffs, 1, cells_y, cells_z), lambda i: (0, jnp.minimum(i, last), 0, 0)),
            pl.BlockSpec((coeffs, 1, beside_y, cells_z), lambda i: (0, jnp.minimum(i, last), 0, 0)),
            pl.BlockSpec((1, pitch_y * 8, coeffs), lambda i: (jnp.minimum(i, last), 0, 0)),
        ],
        out_specs=[
            pl.BlockSpec((coeffs, count), lambda i: (0, 0)),
            pl.BlockSpec((others, coeffs, count), lambda i: (0, 0, 0)),
        ],
        out_shape=[
            jax.ShapeDtypeStruct((coeffs, count), jnp.float32),
            jax.ShapeDtypeStruct((others, coeffs, count), jnp.bfloat16),
        ],
        scratch_shapes=[
            pltpu.VMEM((cells_x * plane_cells + 8, LANES), jnp.float32),
            pltpu.VMEM((cells_z // LANES, round_up(coeffs, 8) * cells_y, LANES), jnp.float32),
            pltpu.VMEM((cells_z // LANES, round_up(coeffs, 8) * beside_y, LANES), jnp.float32),
            pltpu.VMEM((count, LANES), jnp.float32),
            pltpu.VMEM((reach, LANES, LANES), jnp.float32),
            pltpu.VMEM((LANES, LANES), jnp.float32),
        ],
        compiler_params=pltpu.CompilerParams(vmem_limit_bytes=60 * 1024 * 1024),
    )(
        jnp.concatenate(cells),
        jnp.concatenate(slots),
        jnp.stack(factors),
        field,
        beside,
        edge,
    )
    total = own
    for i, by in enumerate(offsets[1:]):
        total = total + shifted(other[i], "gx", -by).astype(jnp.float32)
    outgoing = total.astype(jnp.bfloat16)
    routed = lax.all_to_all(outgoing, ("gx", "gy", "gz"), split_axis=1, concat_axis=1, tiled=True)

    block = min(2048, count)
    results = []
    for start in range(0, count, block):
        columns = slice(start, start + block)
        transfer_dirs = jnp.dot(basis, transfer[:, columns], preferred_element_type=jnp.float32)
        shadow_dirs = jnp.dot(basis, routed[:, columns], preferred_element_type=jnp.float32)
        product = (transfer_dirs * shadow_dirs).astype(jnp.bfloat16)
        results.append(
            jnp.dot(projector, product, preferred_element_type=jnp.float32).astype(jnp.bfloat16)
        )
    return jnp.concatenate(results, axis=1)


def solution(mesh):
    placed = (
        P(None, "gx", "gy", "gz"),
        P(None, None, ("gx", "gy", "gz")),
        P(None, ("gx", "gy", "gz")),
        P(None, ("gx", "gy", "gz")),
        P(None, ("gx", "gy", "gz")),
    )
    return jax.shard_map(
        per_device,
        mesh=mesh,
        in_specs=placed,
        out_specs=P(None, ("gx", "gy", "gz")),
        check_vma=False,
    )
```
